32 devices in a mesh: group: 8 (over z, x), member: 4 (over y, core).
Axes of the slice: x: 2, y: 2, z: 4, core: 2. Of those that a mesh axis runs over, the one named last changes fastest.
Arguments:
- queries: float32 [16384, 256], P(('group', 'member')), may hold values from -6 to 6
- keys: float32 [16384, 256], P(('group', 'member')), may hold values from -6 to 6
- values: float32 [16384, 256], P(('group', 'member')), may hold values from -6 to 6
- outputs: float32 [16384, 256], P(('group', 'member')), may hold values from -3 to 3
- out_grads: float32 [16384, 256], P(('group', 'member')), may hold values from -96 to 96
- log_sums: float32 [16384, 2], P(('group', 'member')), may hold values from 7.5 to 8.75
- block_lists: int32 [128, 8], P(('group', 'member')), may hold values from 0 to 127, as said below
Outputs:
- query_grads: float32 [16384, 256], P(('group', 'member'))
- key_grads: float32 [16384, 256], P(('group', 'member'))
- value_grads: float32 [16384, 256], P(('group', 'member'))
The draws below stay inside these ranges and needn't reach their ends.
Inputs may be any that keep to these rules, and one draw needn't show every extreme that they name: `block_lists`: block b lies on device b // 4, which is in group b // 16 at member (b // 4) % 4; group numbers are taken cyclically modulo 8. Row b lists 8 distinct blocks: first b, then the other blocks of its own device, then all 4 blocks of the one other device, each in group g - 1, g or g + 1 of b's group g. Whether a block of member m lists the blocks of member m2, and in which group offset, depends on m and m2 only (the offset is never 0 when m2 = m), and for each m exactly 4 members m2 are listed by one of m's blocks, so that of the blocks of member m in groups t - 1, t, t + 1 exactly one lists the device of group t at member m2 for each such m2.
All inputs are finite; a program needn't handle non-finite values.
Results may differ from the reference program's by a relative error of at most 0.0003.
Values sent between devices are 32-bit elements; how exact they have to be, the bound alone decides.
A program may use at most 64 MiB of HBM per device.

```python
import jax
import jax.numpy as jnp
from jax import lax

HEAD_DIM = 128
HEADS = 2
BLK = 128
BPD = 4
LIST = 8
NBLK = 128
TOKENS = 16384
N_GROUP = 8
N_MEMBER = 4


def draw_block_lists(key, part):
    key_one, key_two, key_three, key_four = jax.random.split(jax.random.fold_in(key, 11), 4)
    remote_count = min(3, N_MEMBER // BPD)
    used_count = BPD * remote_count
    members = jnp.arange(N_MEMBER, dtype=jnp.int32)
    groups = jnp.arange(N_GROUP, dtype=jnp.int32)
    pick_scores = jax.random.randint(key_one, (N_MEMBER, N_MEMBER), 0, 1 << 20).astype(jnp.int32) * N_MEMBER + members[None, :]
    pick_rank = jnp.sum((pick_scores[:, None, :] < pick_scores[:, :, None]).astype(jnp.int32), axis=2)
    used = pick_rank < used_count
    offset = jax.random.randint(key_two, (N_MEMBER, N_MEMBER), 0, 3).astype(jnp.int32) - 1
    flipped = 1 - 2 * jax.random.randint(key_three, (N_MEMBER, N_MEMBER), 0, 2).astype(jnp.int32)
    diagonal = members[:, None] == members[None, :]
    offset = jnp.where(diagonal & (offset == 0), flipped, offset)
    order_scores = jax.random.randint(key_four, (N_GROUP, N_MEMBER, N_MEMBER), 0, 1 << 20).astype(jnp.int32) * N_MEMBER + members[None, None, :]
    masked = jnp.where(used[None, :, :], order_scores, 1 << 30)
    order_rank = jnp.sum((masked[:, :, None, :] < masked[:, :, :, None]).astype(jnp.int32), axis=3)
    slot_block = order_rank // remote_count
    block_index = jnp.arange(BPD, dtype=jnp.int32)
    listed = used[None, :, None, :] & (slot_block[:, :, None, :] == block_index[None, None, :, None])
    ranked = jnp.where(listed, N_MEMBER - members[None, None, None, :], -1)
    chosen = lax.top_k(ranked, remote_count)[1].astype(jnp.int32)
    chosen_offset = offset[members[None, :, None, None], chosen]
    chosen_group = (groups[:, None, None, None] + chosen_offset + N_GROUP) % N_GROUP
    chosen_device = chosen_group * N_MEMBER + chosen
    remote_blocks = (chosen_device[..., None] * BPD + block_index).reshape(N_GROUP, N_MEMBER, BPD, remote_count * BPD)
    own_device = groups[:, None] * N_MEMBER + members[None, :]
    own_blocks = own_device[:, :, None, None] * BPD + (block_index[:, None] + block_index[None, :]) % BPD
    own_blocks = jnp.broadcast_to(own_blocks, (N_GROUP, N_MEMBER, BPD, BPD))
    lists = jnp.concatenate([own_blocks, remote_blocks], axis=3)
    return lists.reshape(NBLK, LIST).astype(jnp.int32)


def shard_levels(key, extent, cuts, low, top_value):
    loudness, own = 1.0, jax.random.fold_in(key, 6)
    for position, parts in cuts:
        heights = jnp.exp(jax.random.uniform(jax.random.fold_in(own, position), (parts,), jnp.float32, low / len(cuts), top_value / len(cuts)))
        loudness = loudness * jnp.repeat(heights, extent[position] // parts).reshape([-1 if axis == position else 1 for axis in range(len(extent))])
    return loudness


def normal_values(rng, shape, deviation, reach, cuts=(), held_as=jnp.bfloat16):
    array = jax.random.normal(rng, shape, jnp.float32) * deviation
    if len(cuts) > 0:
        array = shard_levels(rng, shape, cuts, -0.22, 0.18) * array
    return jnp.clip(array, min=-reach, max=reach).astype(held_as)


def setup_inputs(seed: int = 0) -> dict:
    seeds = jax.random.split(jax.random.key(seed), 8)
    queries = normal_values(seeds[0], (TOKENS, HEADS * HEAD_DIM), 1.0, 6.0, ((0, 32),), jnp.float32)
    keys = normal_values(seeds[1], (TOKENS, HEADS * HEAD_DIM), 1.0, 6.0, ((0, 32),), jnp.float32)
    values = normal_values(seeds[2], (TOKENS, HEADS * HEAD_DIM), 1.0, 6.0, ((0, 32),), jnp.float32)
    outputs = normal_values(seeds[3], (TOKENS, HEADS * HEAD_DIM), 0.5, 3.0, ((0, 32),), jnp.float32)
    out_grads = normal_values(seeds[4], (TOKENS, HEADS * HEAD_DIM), 16.0, 96.0, ((0, 32),), jnp.float32)
    log_sums = jnp.clip(7.5 + 1.25 * jax.random.uniform(seeds[5], (TOKENS, HEADS), jnp.float32) ** shard_levels(seeds[5], (TOKENS, HEADS), ((0, 32),), -0.2, 0.2), 7.5, 8.75)
    block_lists = draw_block_lists(jax.random.fold_in(seeds[7], 71), 0)
    return {"queries": queries, "keys": keys, "values": values, "outputs": outputs, "out_grads": out_grads, "log_sums": log_sums, "block_lists": block_lists}


exact_mode = lax.Precision.HIGHEST


def reference(queries, keys, values, outputs, out_grads, log_sums, block_lists):
    score_scale = HEAD_DIM ** -0.5
    shape_four = (NBLK, BLK, HEADS, HEAD_DIM)
    query_all = queries.reshape(shape_four)
    key_all = keys.reshape(shape_four)
    value_all = values.reshape(shape_four)
    grad_all = out_grads.reshape(shape_four)
    row_delta = jnp.sum(grad_all * outputs.reshape(shape_four), axis=3)
    lse_all = log_sums.reshape(NBLK, BLK, HEADS)

    def one_block(totals, block_index):
        key_total, value_total = totals
        key_ids = block_lists[block_index].astype(jnp.int32)
        key_rows = key_all[key_ids]
        value_rows = value_all[key_ids]
        query_rows = query_all[block_index]
        grad_rows = grad_all[block_index]
        scores = jnp.einsum("qhd,jkhd->hqjk", query_rows, key_rows, precision=exact_mode) * score_scale
        weights = jnp.exp(scores - lse_all[block_index].T[:, :, None, None])
        value_part = jnp.einsum("hqjk,qhd->jkhd", weights, grad_rows, precision=exact_mode)
        prob_grads = jnp.einsum("qhd,jkhd->hqjk", grad_rows, value_rows, precision=exact_mode)
        score_grads = weights * (prob_grads - row_delta[block_index].T[:, :, None, None])
        query_part = jnp.einsum("hqjk,jkhd->qhd", score_grads, key_rows, precision=exact_mode) * score_scale
        key_part = jnp.einsum("hqjk,qhd->jkhd", score_grads, query_rows, precision=exact_mode) * score_scale
        return (key_total.at[key_ids].add(key_part), value_total.at[key_ids].add(value_part)), query_part

    zeros_all = jnp.zeros(shape_four, queries.dtype)
    (key_total, value_total), query_total = lax.scan(one_block, (zeros_all, zeros_all), jnp.arange(NBLK, dtype=jnp.int32))
    width_all = HEADS * HEAD_DIM
    return (query_total.reshape(TOKENS, width_all), key_total.reshape(TOKENS, width_all), value_total.reshape(TOKENS, width_all))
```

```python
import functools

import jax
import jax.numpy as jnp
from jax import lax
from jax.experimental import pallas as pl
from jax.experimental.pallas import tpu as pltpu
from jax.sharding import PartitionSpec as P

MESH = pl.DeviceIdType.MESH
UNLISTED = 2.0


def split(x):
    high = x.astype(jnp.bfloat16)
    return high, (x - high.astype(jnp.float32)).astype(jnp.bfloat16)


def dot(a, b):
    return lax.dot_general(a, b, (((1,), (0,)), ((), ())), preferred_element_type=jnp.float32)


def dot_t(a, b):
    return lax.dot_general(a, b, (((1,), (1,)), ((), ())), preferred_element_type=jnp.float32)


def xor_index(a, b, count):
    total, bit = 0, 1
    while bit < count:
        total = total + ((a // bit + b // bit) % 2) * bit
        bit *= 2
    return total


def kernel(
    sizes, table_ref, q_ref, k_ref, v_ref, o_ref, g_ref, lse_ref, dq_ref, dk_ref, dv_ref,
    kcat, vcat, ktcat, meta, stage, m_arr, x_arr, z_arr, item, dq_slot, z_ret, x_out, x_ret, m_out, m_ret,
    m_sems, x_sems, z_sems, zr_sems, xr_sems, mr_sems,
):
    groups, members, heads, width, blocks, rows = sizes
    scale = width ** -0.5
    group, member = lax.axis_index("group"), lax.axis_index("member")
    parity = group % 2
    partner = group + 1 - 2 * parity
    far_to = (group + 2 - 4 * parity + groups) % groups
    far_from = (group - 2 + 4 * parity + groups) % groups
    near_flag = (2 * parity - 1).astype(jnp.float32)

    barrier = pltpu.get_barrier_semaphore()
    for other in (partner, far_to, far_from):
        pl.semaphore_signal(barrier, inc=1, device_id=(other, member), device_id_type=MESH)
    for step in range(1, members):
        pl.semaphore_signal(
            barrier, inc=1, device_id=(group, xor_index(member, step, members)), device_id_type=MESH
        )

    def remote(source, target, sems, slot, device):
        return pltpu.make_async_remote_copy(
            src_ref=source.at[slot], dst_ref=target.at[slot],
            send_sem=sems.at[0, slot], recv_sem=sems.at[1, slot],
            device_id=device, device_id_type=MESH,
        )

    def member_of(slot):
        return (group, xor_index(member, slot, members))

    eye = lax.broadcasted_iota(jnp.int32, (rows, rows), 0) == lax.broadcasted_iota(
        jnp.int32, (rows, rows), 1
    )

    def as_row(column):
        return jnp.sum(jnp.where(eye, column, 0.0), axis=0, keepdims=True)

    for b in range(blocks):
        here = pl.ds(b * rows, rows)
        meta[b] = jnp.zeros((8, heads * width), jnp.float32)
        for h in range(heads):
            cols = pl.ds(h * width, width)
            meta[b, 0:1, cols] = as_row(lse_ref[here, h : h + 1])
            delta = jnp.sum(g_ref[here, cols] * o_ref[here, cols], axis=1, keepdims=True)
            meta[b, 1:2, cols] = as_row(delta)

    for slot in range(members):
        def picked(read):
            return sum(read(b) * table_ref[slot, b] for b in range(blocks))

        stage[slot, 0:rows, :] = picked(lambda b: q_ref[pl.ds(b * rows, rows), :])
        stage[slot, rows : 2 * rows, :] = picked(lambda b: g_ref[pl.ds(b * rows, rows), :])
        stage[slot, 2 * rows : 2 * rows + 8, :] = picked(lambda b: meta[b])
        stage[slot, 2 * rows + 2 : 2 * rows + 3, :] = jnp.full(
            (1, heads * width), table_ref[slot, blocks]
        )

    pl.semaphore_wait(barrier, members + 2)
    remote(stage, x_arr, x_sems, 0, (partner, member)).start()
    for slot in range(1, members):
        remote(stage, m_arr, m_sems, slot, member_of(slot)).start()

    for h in range(heads):
        cols = pl.ds(h * width, width)
        kh, kl = split(k_ref[:, cols])
        kcat[h, :, 0:width] = kh
        kcat[h, :, width : 2 * width] = kl
        vh, vl = split(v_ref[:, cols])
        vcat[h, :, 0:width] = vh
        vcat[h, :, width : 2 * width] = vl
        th, tl = split(k_ref[:, cols].T)
        ktcat[h, 0:width, :] = th
        ktcat[h, width : 2 * width, :] = tl
    dk_ref[...] = jnp.zeros_like(dk_ref)
    dv_ref[...] = jnp.zeros_like(dv_ref)

    def attend(q, g, lse, delta, h):
        cols = pl.ds(h * width, width)
        qh, ql = split(q)
        gh, gl = split(g)
        kh, vh = kcat[h, :, 0:width], vcat[h, :, 0:width]
        scores = dot_t(kcat[h], jnp.concatenate([qh, qh], axis=1)) + dot_t(kh, ql)
        weights = jnp.exp(scores * scale - lse)
        prob_grads = dot_t(vcat[h], jnp.concatenate([gh, gh], axis=1)) + dot_t(vh, gl)
        score_grads = weights * (prob_grads - delta)
        ph, plow = split(weights)
        dv_ref[:, cols] += dot(jnp.concatenate([ph, plow], axis=1), jnp.concatenate([gh, gh], axis=0)) + dot(ph, gl)
        sh, sl = split(score_grads)
        dk_ref[:, cols] += dot(jnp.concatenate([sh, sl], axis=1), jnp.concatenate([qh, qh], axis=0)) + dot(sh, ql)
        kth, ktl = ktcat[h, 0:width, :], ktcat[h, width : 2 * width, :]
        dqt = dot(kth, sh) + dot(ktl, sh) + dot(kth, sl)
        return dqt.T * scale

    def own_block(b):
        here = pl.ds(pl.multiple_of(b * rows, rows), rows)
        for h in range(heads):
            cols = pl.ds(h * width, width)
            dq_ref[here, cols] = attend(
                q_ref[here, cols], g_ref[here, cols], meta[b, 0:1, cols], meta[b, 1:2, cols], h
            )

    def forward_member(slot):
        remote(stage, m_arr, m_sems, slot, member_of(slot)).wait_recv()
        remote(m_arr, x_arr, x_sems, slot, (partner, member)).start()

    def forward_far(slot):
        remote(stage, x_arr, x_sems, slot, (partner, member)).wait_recv()
        remote(x_arr, z_arr, z_sems, slot, (far_to, member)).start()

    own_block(0)
    for slot in range(1, members):
        forward_member(slot)
        if slot == 1:
            forward_far(0)
        if slot < blocks:
            own_block(slot)
    for b in range(max(members, 1), blocks):
        own_block(b)

    def local_of(slot):
        return stage if slot == 0 else m_arr

    flag_row = 2 * rows + 2

    def return_far(slot):
        remote(dq_slot, z_ret, zr_sems, slot, (far_from, member)).wait_recv()
        flag = local_of(slot)[slot, flag_row : flag_row + 1, :]
        x_out[slot] = jnp.where(flag == near_flag, dq_slot[slot], z_ret[slot])
        remote(x_out, x_ret, xr_sems, slot, (partner, member)).start()

    def return_near(slot):
        remote(x_out, x_ret, xr_sems, slot, (partner, member)).wait_recv()
        flag = local_of(slot)[slot, flag_row : flag_row + 1, :]
        total = jnp.where(flag == 0.0, dq_slot[slot], x_ret[slot])
        if slot == 0:
            m_ret[0] = total
        else:
            m_out[slot] = total
            remote(m_out, m_ret, mr_sems, slot, member_of(slot)).start()

    for slot in range(members):
        if slot + 1 < members:
            forward_far(slot + 1)
        remote(x_arr, z_arr, z_sems, slot, (far_to, member)).wait_recv()
        local = local_of(slot)
        flag = local[slot, flag_row : flag_row + 1, :]
        item[...] = jnp.where(
            flag == 0.0, local[slot], jnp.where(flag == near_flag, x_arr[slot], z_arr[slot])
        )
        for h in range(heads):
            cols = pl.ds(h * width, width)
            lse = jnp.where(flag[:, 0:width] == UNLISTED, 1e30, item[2 * rows : 2 * rows + 1, cols])
            dq_slot[slot, :, cols] = attend(
                item[0:rows, cols], item[rows : 2 * rows, cols], lse,
                item[2 * rows + 1 : 2 * rows + 2, cols], h,
            )
        remote(dq_slot, z_ret, zr_sems, slot, (far_from, member)).start()
        if slot >= 1:
            return_far(slot - 1)
        if slot >= 2:
            return_near(slot - 2)
    dk_ref[...] = dk_ref[...] * scale
    return_far(members - 1)
    for slot in range(max(members - 2, 0), members):
        return_near(slot)
    for slot in range(members):
        if slot >= 1:
            remote(m_out, m_ret, mr_sems, slot, member_of(slot)).wait_recv()
        for b in range(blocks):
            here = pl.ds(b * rows, rows)
            dq_ref[here, :] += m_ret[slot] * table_ref[slot, b]

    for slot in range(members):
        remote(local_of(slot), x_arr, x_sems, slot, (partner, member)).wait_send()
        remote(x_arr, z_arr, z_sems, slot, (far_to, member)).wait_send()
        remote(dq_slot, z_ret, zr_sems, slot, (far_from, member)).wait_send()
        remote(x_out, x_ret, xr_sems, slot, (partner, member)).wait_send()
        if slot >= 1:
            remote(stage, m_arr, m_sems, slot, member_of(slot)).wait_send()
            remote(m_out, m_ret, mr_sems, slot, member_of(slot)).wait_send()


def slot_table(block_lists, groups, members):
    blocks = block_lists.shape[0]
    group, member = lax.axis_index("group"), lax.axis_index("member")
    target = member ^ jnp.arange(members, dtype=jnp.int32)
    device = block_lists[:, blocks:] // blocks
    hit = (device % members)[None] == target[:, None, None]
    offset = (device // members - group + 1 + groups) % groups - 1
    flag = jnp.max(jnp.where(hit, offset[None], -groups), axis=(1, 2))
    flag = jnp.where(flag == -groups, UNLISTED, flag.astype(jnp.float32))
    return jnp.concatenate([jnp.any(hit, axis=2).astype(jnp.float32), flag[:, None]], axis=1)


def body(queries, keys, values, outputs, out_grads, log_sums, block_lists):
    tokens, width_all = queries.shape
    heads = log_sums.shape[1]
    blocks = block_lists.shape[0]
    rows, width = tokens // blocks, width_all // heads
    groups, members = lax.axis_size("group"), lax.axis_size("member")
    sizes = (groups, members, heads, width, blocks, rows)
    vmem = pl.BlockSpec(memory_space=pltpu.VMEM)
    packed = pltpu.VMEM((members, 2 * rows + 8, width_all), jnp.float32)
    terms = pltpu.VMEM((members, rows, width_all), jnp.float32)
    sems = pltpu.SemaphoreType.DMA((2, members))
    return pl.pallas_call(
        functools.partial(kernel, sizes),
        out_shape=[jax.ShapeDtypeStruct((tokens, width_all), jnp.float32)] * 3,
        in_specs=[pl.BlockSpec(memory_space=pltpu.SMEM)] + [vmem] * 6,
        out_specs=[vmem] * 3,
        scratch_shapes=[
            pltpu.VMEM((heads, tokens, 2 * width), jnp.bfloat16),
            pltpu.VMEM((heads, tokens, 2 * width), jnp.bfloat16),
            pltpu.VMEM((heads, 2 * width, tokens), jnp.bfloat16),
            pltpu.VMEM((blocks, 8, width_all), jnp.float32),
            packed, packed, packed, packed,
            pltpu.VMEM((2 * rows + 8, width_all), jnp.float32),
            terms, terms, terms, terms, terms, terms,
            sems, sems, sems, sems, sems, sems,
        ],
        compiler_params=pltpu.CompilerParams(
            collective_id=0, has_side_effects=True, vmem_limit_bytes=60 * 1024 * 1024
        ),
    )(slot_table(block_lists, groups, members), queries, keys, values, outputs, out_grads, log_sums)


def solution(mesh):
    spec = P(("group", "member"), None)
    return jax.shard_map(
        body, mesh=mesh, in_specs=(spec,) * 7, out_specs=(spec,) * 3, check_vma=False
    )
```

```python
import functools

import jax
import jax.numpy as jnp
from jax import lax
from jax.experimental import pallas as pl
from jax.experimental.pallas import tpu as pltpu
from jax.sharding import PartitionSpec as P

MESH = pl.DeviceIdType.MESH
UNLISTED = 2.0


def split(x):
    high = x.astype(jnp.bfloat16)
    return high, (x - high.astype(jnp.float32)).astype(jnp.bfloat16)


def dot(a, b):
    return lax.dot_general(a, b, (((1,), (0,)), ((), ())), preferred_element_type=jnp.float32)


def dot_t(a, b):
    return lax.dot_general(a, b, (((1,), (1,)), ((), ())), preferred_element_type=jnp.float32)


def xor_index(a, b, count):
    total, bit = 0, 1
    while bit < count:
        total = total + ((a // bit + b // bit) % 2) * bit
        bit *= 2
    return total


def kernel(
    sizes, table_ref, q_ref, k_hbm, v_hbm, o_ref, g_ref, lse_ref, dq_ref, dk_ref, dv_ref,
    k_ref, v_ref, kcat, vcat, ktcat, meta, stage, m_arr, x_arr, z_arr, item,
    dq_item, z_ret, x_out, x_ret, m_out, m_ret,
    kv_sems, m_sems, x_sems, z_sems, zr_sems, xr_sems, mr_sems,
):
    groups, members, heads, width, blocks, rows = sizes
    scale = width ** -0.5
    group, member = lax.axis_index("group"), lax.axis_index("member")
    parity = group % 2
    partner = group + 1 - 2 * parity
    far_to = (group + 2 - 4 * parity + groups) % groups
    far_from = (group - 2 + 4 * parity + groups) % groups
    near_flag = (2 * parity - 1).astype(jnp.float32)

    barrier = pltpu.get_barrier_semaphore()
    for other in (partner, far_to, far_from):
        pl.semaphore_signal(barrier, inc=1, device_id=(other, member), device_id_type=MESH)
    for step in range(1, members):
        pl.semaphore_signal(
            barrier, inc=1, device_id=(group, xor_index(member, step, members)), device_id_type=MESH
        )
    kv_copies = [
        pltpu.make_async_copy(k_hbm, k_ref, kv_sems.at[0]),
        pltpu.make_async_copy(v_hbm, v_ref, kv_sems.at[1]),
    ]
    for copy in kv_copies:
        copy.start()

    slots = [0] + list(range(2, members)) + list(range(1, min(members, 2)))
    items = [(slot, h) for slot in slots for h in range(heads)]
    count = len(items)

    def remote(source, target, sems, n, device):
        return pltpu.make_async_remote_copy(
            src_ref=source.at[n], dst_ref=target.at[n],
            send_sem=sems.at[0, n], recv_sem=sems.at[1, n],
            device_id=device, device_id_type=MESH,
        )

    def to_member(source, target, sems, n):
        return remote(source, target, sems, n, (group, xor_index(member, items[n][0], members)))

    def to_partner(source, target, sems, n):
        return remote(source, target, sems, n, (partner, member))

    eye = lax.broadcasted_iota(jnp.int32, (rows, rows), 0) == lax.broadcasted_iota(
        jnp.int32, (rows, rows), 1
    )
    for b in range(blocks):
        here = pl.ds(b * rows, rows)
        for h in range(heads):
            cols = pl.ds(h * width, width)
            delta = jnp.sum(g_ref[here, cols] * o_ref[here, cols], axis=1, keepdims=True)
            meta[b, h, 0:1, :] = lse_ref[h : h + 1, here]
            meta[b, h, 1:2, :] = jnp.sum(jnp.where(eye, delta, 0.0), axis=0, keepdims=True)

    def fill(n):
        slot, h = items[n]
        cols = pl.ds(h * width, width)

        def picked(read):
            return sum(read(b) * table_ref[slot, b] for b in range(blocks))

        stage[n, 0:rows, :] = picked(lambda b: q_ref[pl.ds(b * rows, rows), cols])
        stage[n, rows : 2 * rows, :] = picked(lambda b: g_ref[pl.ds(b * rows, rows), cols])
        stage[n, 2 * rows : 2 * rows + 2, :] = picked(lambda b: meta[b, h, 0:2, :])
        stage[n, 2 * rows + 2 : 2 * rows + 8, :] = jnp.full((6, width), table_ref[slot, blocks])

    for n in range(count):
        if n <= heads:
            fill(n)
    pl.semaphore_wait(barrier, members + 2)
    for n in range(count):
        if n > heads:
            fill(n)
        if items[n][0] == 0:
            to_partner(stage, x_arr, x_sems, n).start()
        else:
            to_member(stage, m_arr, m_sems, n).start()

    for copy in kv_copies:
        copy.wait()
    for h in range(heads):
        cols = pl.ds(h * width, width)
        kh, kl = split(k_ref[:, cols])
        kcat[h, :, 0:width] = kh
        kcat[h, :, width : 2 * width] = kl
        vh, vl = split(v_ref[:, cols])
        vcat[h, :, 0:width] = vh
        vcat[h, :, width : 2 * width] = vl
        th, tl = split(k_ref[:, cols].T)
        ktcat[h, 0:width, :] = th
        ktcat[h, width : 2 * width, :] = tl
    dk_ref[...] = jnp.zeros_like(dk_ref)
    dv_ref[...] = jnp.zeros_like(dv_ref)

    def attend(q, g, lse, delta, h):
        cols = pl.ds(h * width, width)
        qh, ql = split(q)
        gh, gl = split(g)
        kh, vh = kcat[h, :, 0:width], vcat[h, :, 0:width]
        scores = dot_t(kcat[h], jnp.concatenate([qh, qh], axis=1)) + dot_t(kh, ql)
        weights = jnp.exp(scores * scale - lse)
        prob_grads = dot_t(vcat[h], jnp.concatenate([gh, gh], axis=1)) + dot_t(vh, gl)
        score_grads = weights * (prob_grads - delta)
        ph, plow = split(weights)
        dv_ref[:, cols] += dot(
            jnp.concatenate([ph, plow], axis=1), jnp.concatenate([gh, gh], axis=0)
        ) + dot(ph, gl)
        sh, sl = split(score_grads)
        dk_ref[:, cols] += dot(
            jnp.concatenate([sh, sl], axis=1), jnp.concatenate([qh, qh], axis=0)
        ) + dot(sh, ql)
        kth, ktl = ktcat[h, 0:width, :], ktcat[h, width : 2 * width, :]
        return (dot(kth, sh) + dot(ktl, sh) + dot(kth, sl)).T * scale

    def own_unit(unit):
        b, h = unit // heads, unit % heads
        here, cols = pl.ds(b * rows, rows), pl.ds(h * width, width)
        dq_ref[here, cols] = attend(
            q_ref[here, cols], g_ref[here, cols], meta[b, h, 0:1, :], meta[b, h, 1:2, :], h
        )

    def local_of(n):
        return stage if items[n][0] == 0 else m_arr

    def flag_of(n):
        return local_of(n)[n, 2 * rows + 2 : 2 * rows + 3, :]

    def forward_member(n):
        if items[n][0] != 0:
            to_member(stage, m_arr, m_sems, n).wait_recv()
            to_partner(m_arr, x_arr, x_sems, n).start()

    def forward_far(n):
        to_partner(stage, x_arr, x_sems, n).wait_recv()
        remote(x_arr, z_arr, z_sems, n, (far_to, member)).start()

    def compute(n):
        remote(x_arr, z_arr, z_sems, n, (far_to, member)).wait_recv()
        flag = flag_of(n)
        item[...] = jnp.where(
            flag == 0.0, local_of(n)[n], jnp.where(flag == near_flag, x_arr[n], z_arr[n])
        )
        lse = jnp.where(flag == UNLISTED, 1e30, item[2 * rows : 2 * rows + 1, :])
        dq_item[n] = attend(
            item[0:rows, :], item[rows : 2 * rows, :], lse,
            item[2 * rows + 1 : 2 * rows + 2, :], items[n][1],
        )
        remote(dq_item, z_ret, zr_sems, n, (far_from, member)).start()

    def return_far(n):
        remote(dq_item, z_ret, zr_sems, n, (far_from, member)).wait_recv()
        x_out[n] = jnp.where(flag_of(n) == near_flag, dq_item[n], z_ret[n])
        to_partner(x_out, x_ret, xr_sems, n).start()

    def return_near(n):
        to_partner(x_out, x_ret, xr_sems, n).wait_recv()
        total = jnp.where(flag_of(n) == 0.0, dq_item[n], x_ret[n])
        if items[n][0] == 0:
            m_ret[n] = total
        else:
            m_out[n] = total
            to_member(m_out, m_ret, mr_sems, n).start()

    def finish(n):
        slot, h = items[n]
        if slot != 0:
            to_member(m_out, m_ret, mr_sems, n).wait_recv()
        for b in range(blocks):
            here, cols = pl.ds(b * rows, rows), pl.ds(h * width, width)
            dq_ref[here, cols] += m_ret[n] * table_ref[slot, b]

    units = blocks * heads
    stages = ((forward_member, -1), (forward_far, 1), (compute, 2), (return_far, 4), (return_near, 6), (finish, 8))
    for step in range(-1, max(count + 9, units)):
        if 0 <= step < units:
            own_unit(step)
        for stage_of, lag in stages:
            if 0 <= step - lag < count:
                stage_of(step - lag)
        if step == count + 1:
            dk_ref[...] = dk_ref[...] * scale

    for n in range(count):
        to_partner(local_of(n), x_arr, x_sems, n).wait_send()
        remote(x_arr, z_arr, z_sems, n, (far_to, member)).wait_send()
        remote(dq_item, z_ret, zr_sems, n, (far_from, member)).wait_send()
        to_partner(x_out, x_ret, xr_sems, n).wait_send()
        if items[n][0] != 0:
            to_member(stage, m_arr, m_sems, n).wait_send()
            to_member(m_out, m_ret, mr_sems, n).wait_send()


def slot_table(block_lists, groups, members):
    blocks = block_lists.shape[0]
    group, member = lax.axis_index("group"), lax.axis_index("member")
    target = member ^ jnp.arange(members, dtype=jnp.int32)
    device = block_lists[:, blocks:] // blocks
    hit = (device % members)[None] == target[:, None, None]
    offset = (device // members - group + 1 + groups) % groups - 1
    flag = jnp.max(jnp.where(hit, offset[None], -groups), axis=(1, 2))
    flag = jnp.where(flag == -groups, UNLISTED, flag.astype(jnp.float32))
    return jnp.concatenate([jnp.any(hit, axis=2).astype(jnp.float32), flag[:, None]], axis=1)


def body(queries, keys, values, outputs, out_grads, log_sums, block_lists):
    tokens, width_all = queries.shape
    heads = log_sums.shape[1]
    blocks = block_lists.shape[0]
    rows, width = tokens // blocks, width_all // heads
    groups, members = lax.axis_size("group"), lax.axis_size("member")
    sizes = (groups, members, heads, width, blocks, rows)
    vmem = pl.BlockSpec(memory_space=pltpu.VMEM)
    anywhere = pl.BlockSpec(memory_space=pl.ANY)
    count = members * heads
    packed = pltpu.VMEM((count, 2 * rows + 8, width), jnp.float32)
    terms = pltpu.VMEM((count, rows, width), jnp.float32)
    sems = pltpu.SemaphoreType.DMA((2, count))
    return pl.pallas_call(
        functools.partial(kernel, sizes),
        out_shape=[jax.ShapeDtypeStruct((tokens, width_all), jnp.float32)] * 3,
        in_specs=[pl.BlockSpec(memory_space=pltpu.SMEM), vmem, anywhere, anywhere, vmem, vmem, vmem],
        out_specs=[vmem] * 3,
        scratch_shapes=[
            pltpu.VMEM((tokens, width_all), jnp.float32),
            pltpu.VMEM((tokens, width_all), jnp.float32),
            pltpu.VMEM((heads, tokens, 2 * width), jnp.bfloat16),
            pltpu.VMEM((heads, tokens, 2 * width), jnp.bfloat16),
            pltpu.VMEM((heads, 2 * width, tokens), jnp.bfloat16),
            pltpu.VMEM((blocks, heads, 8, width), jnp.float32),
            packed, packed, packed, packed,
            pltpu.VMEM((2 * rows + 8, width), jnp.float32),
            terms, terms, terms, terms, terms, terms,
            pltpu.SemaphoreType.DMA((2,)),
            sems, sems, sems, sems, sems, sems,
        ],
        compiler_params=pltpu.CompilerParams(
            collective_id=0, has_side_effects=True, vmem_limit_bytes=60 * 1024 * 1024
        ),
    )(slot_table(block_lists, groups, members), queries, keys, values, outputs, out_grads, log_sums.T)


def solution(mesh):
    spec = P(("group", "member"), None)
    return jax.shard_map(
        body, mesh=mesh, in_specs=(spec,) * 7, out_specs=(spec,) * 3, check_vma=False
    )
```

```python
import functools

import jax
import jax.numpy as jnp
from jax import lax
from jax.experimental import pallas as pl
from jax.experimental.pallas import tpu as pltpu
from jax.sharding import PartitionSpec as P

MESH = pl.DeviceIdType.MESH
UNLISTED = 2.0


def split(x):
    high = x.astype(jnp.bfloat16)
    return high, (x - high.astype(jnp.float32)).astype(jnp.bfloat16)


def dot(a, b):
    return lax.dot_general(a, b, (((1,), (0,)), ((), ())), preferred_element_type=jnp.float32)


def dot_t(a, b):
    return lax.dot_general(a, b, (((1,), (1,)), ((), ())), preferred_element_type=jnp.float32)


def xor_index(a, b, count):
    total, bit = 0, 1
    while bit < count:
        total = total + ((a // bit + b // bit) % 2) * bit
        bit *= 2
    return total


def kernel(
    sizes, lists_ref, q_hbm, k_hbm, v_hbm, o_hbm, g_hbm, lse_ref, dq_ref, dk_ref, dv_ref,
    q_ref, o_ref, g_ref, k_ref, v_ref, kcat, vcat, ktcat, meta, stage, m_arr, x_arr, z_arr, item,
    dq_item, z_ret, x_out, x_ret, m_out, m_ret,
    kv_sems, m_sems, x_sems, z_sems, zr_sems, xr_sems, mr_sems,
):
    groups, members, heads, width, blocks, rows = sizes
    factors, flags = {}, {}
    scale = width ** -0.5
    group, member = lax.axis_index("group"), lax.axis_index("member")
    parity = group % 2
    partner = group + 1 - 2 * parity
    far_to = (group + 2 - 4 * parity + groups) % groups
    far_from = (group - 2 + 4 * parity + groups) % groups
    near_flag = (2 * parity - 1).astype(jnp.float32)

    barrier = pltpu.get_barrier_semaphore()
    for other in (partner, far_to, far_from):
        pl.semaphore_signal(barrier, inc=1, device_id=(other, member), device_id_type=MESH)
    for step in range(1, members):
        pl.semaphore_signal(
            barrier, inc=1, device_id=(group, xor_index(member, step, members)), device_id_type=MESH
        )
    early_copies = [
        pltpu.make_async_copy(g_hbm, g_ref, kv_sems.at[2]),
        pltpu.make_async_copy(o_hbm, o_ref, kv_sems.at[3]),
        pltpu.make_async_copy(q_hbm, q_ref, kv_sems.at[4]),
    ]
    for copy in early_copies:
        copy.start()
    kv_copies = [
        pltpu.make_async_copy(k_hbm, k_ref, kv_sems.at[0]),
        pltpu.make_async_copy(v_hbm, v_ref, kv_sems.at[1]),
    ]
    for copy in kv_copies:
        copy.start()

    slots = [0] + list(range(2, members)) + list(range(1, min(members, 2)))
    items = [(slot, h) for slot in slots for h in range(heads)]
    count = len(items)

    def remote(source, target, sems, n, device):
        return pltpu.make_async_remote_copy(
            src_ref=source.at[n], dst_ref=target.at[n],
            send_sem=sems.at[0, n], recv_sem=sems.at[1, n],
            device_id=device, device_id_type=MESH,
        )

    def to_member(source, target, sems, n):
        return remote(source, target, sems, n, (group, xor_index(member, items[n][0], members)))

    def to_partner(source, target, sems, n):
        return remote(source, target, sems, n, (partner, member))

    listed = lists_ref.shape[1]
    for slot in range(members):
        target = xor_index(member, slot, members)
        flag = jnp.int32(-groups)
        for b in range(blocks):
            hits = jnp.int32(0)
            for entry in range(blocks, listed):
                device = lax.div(lists_ref[b, entry], jnp.int32(blocks))
                hit = lax.rem(device, jnp.int32(members)) == target
                offset = lax.rem(
                    lax.div(device, jnp.int32(members)) - group + 1 + groups, jnp.int32(groups)
                ) - 1
                hits = jnp.maximum(hits, hit.astype(jnp.int32))
                flag = jnp.maximum(flag, jnp.where(hit, offset, -groups))
            factors[slot, b] = hits.astype(jnp.float32)
        flags[slot] = jnp.where(flag == -groups, UNLISTED, flag.astype(jnp.float32))

    for copy in early_copies:
        copy.wait()

    eye = lax.broadcasted_iota(jnp.int32, (rows, rows), 0) == lax.broadcasted_iota(
        jnp.int32, (rows, rows), 1
    )
    for b in range(blocks):
        here = pl.ds(b * rows, rows)
        for h in range(heads):
            cols = pl.ds(h * width, width)
            delta = jnp.sum(g_ref[here, cols] * o_ref[here, cols], axis=1, keepdims=True)
            meta[b, h, 0:1, :] = lse_ref[h : h + 1, here]
            meta[b, h, 1:2, :] = jnp.sum(jnp.where(eye, delta, 0.0), axis=0, keepdims=True)

    def fill(n):
        slot, h = items[n]
        cols = pl.ds(h * width, width)

        def picked(read):
            return sum(read(b) * factors[slot, b] for b in range(blocks))

        stage[n, 0:rows, :] = picked(lambda b: q_ref[pl.ds(b * rows, rows), cols])
        stage[n, rows : 2 * rows, :] = picked(lambda b: g_ref[pl.ds(b * rows, rows), cols])
        stage[n, 2 * rows : 2 * rows + 2, :] = picked(lambda b: meta[b, h, 0:2, :])
        stage[n, 2 * rows + 2 : 2 * rows + 8, :] = jnp.full((6, width), flags[slot])

    for n in range(count):
        if n <= heads:
            fill(n)
    pl.semaphore_wait(barrier, members + 2)
    for n in range(count):
        if n > heads:
            fill(n)
        if items[n][0] == 0:
            to_partner(stage, x_arr, x_sems, n).start()
        else:
            to_member(stage, m_arr, m_sems, n).start()

    for copy in kv_copies:
        copy.wait()
    for h in range(heads):
        cols = pl.ds(h * width, width)
        kh, kl = split(k_ref[:, cols])
        kcat[h, :, 0:width] = kh
        kcat[h, :, width : 2 * width] = kl
        vh, vl = split(v_ref[:, cols])
        vcat[h, :, 0:width] = vh
        vcat[h, :, width : 2 * width] = vl
        th, tl = split(k_ref[:, cols].T)
        ktcat[h, 0:width, :] = th
        ktcat[h, width : 2 * width, :] = tl
    dk_ref[...] = jnp.zeros_like(dk_ref)
    dv_ref[...] = jnp.zeros_like(dv_ref)

    def attend(q, g, lse, delta, h):
        cols = pl.ds(h * width, width)
        qh, ql = split(q)
        gh, gl = split(g)
        kh, vh = kcat[h, :, 0:width], vcat[h, :, 0:width]
        scores = dot_t(kcat[h], jnp.concatenate([qh, qh], axis=1)) + dot_t(kh, ql)
        weights = jnp.exp(scores * scale - lse)
        prob_grads = dot_t(vcat[h], jnp.concatenate([gh, gh], axis=1)) + dot_t(vh, gl)
        score_grads = weights * (prob_grads - delta)
        ph, plow = split(weights)
        dv_ref[:, cols] += dot(
            jnp.concatenate([ph, plow], axis=1), jnp.concatenate([gh, gh], axis=0)
        ) + dot(ph, gl)
        sh, sl = split(score_grads)
        dk_ref[:, cols] += dot(
            jnp.concatenate([sh, sl], axis=1), jnp.concatenate([qh, qh], axis=0)
        ) + dot(sh, ql)
        kth, ktl = ktcat[h, 0:width, :], ktcat[h, width : 2 * width, :]
        return (dot(kth, sh) + dot(ktl, sh) + dot(kth, sl)).T * scale

    def own_unit(unit):
        b, h = unit // heads, unit % heads
        here, cols = pl.ds(b * rows, rows), pl.ds(h * width, width)
        dq_ref[here, cols] = attend(
            q_ref[here, cols], g_ref[here, cols], meta[b, h, 0:1, :], meta[b, h, 1:2, :], h
        )

    def local_of(n):
        return stage if items[n][0] == 0 else m_arr

    def flag_of(n):
        return local_of(n)[n, 2 * rows + 2 : 2 * rows + 3, :]

    def forward_member(n):
        if items[n][0] != 0:
            to_member(stage, m_arr, m_sems, n).wait_recv()
            to_partner(m_arr, x_arr, x_sems, n).start()

    def forward_far(n):
        to_partner(stage, x_arr, x_sems, n).wait_recv()
        remote(x_arr, z_arr, z_sems, n, (far_to, member)).start()

    def compute(n):
        remote(x_arr, z_arr, z_sems, n, (far_to, member)).wait_recv()
        flag = flag_of(n)
        item[...] = jnp.where(
            flag == 0.0, local_of(n)[n], jnp.where(flag == near_flag, x_arr[n], z_arr[n])
        )
        lse = jnp.where(flag == UNLISTED, 1e30, item[2 * rows : 2 * rows + 1, :])
        dq_item[n] = attend(
            item[0:rows, :], item[rows : 2 * rows, :], lse,
            item[2 * rows + 1 : 2 * rows + 2, :], items[n][1],
        )
        remote(dq_item, z_ret, zr_sems, n, (far_from, member)).start()

    def return_far(n):
        remote(dq_item, z_ret, zr_sems, n, (far_from, member)).wait_recv()
        x_out[n] = jnp.where(flag_of(n) == near_flag, dq_item[n], z_ret[n])
        to_partner(x_out, x_ret, xr_sems, n).start()

    def return_near(n):
        to_partner(x_out, x_ret, xr_sems, n).wait_recv()
        total = jnp.where(flag_of(n) == 0.0, dq_item[n], x_ret[n])
        if items[n][0] == 0:
            m_ret[n] = total
        else:
            m_out[n] = total
            to_member(m_out, m_ret, mr_sems, n).start()

    def finish(n):
        slot, h = items[n]
        if slot != 0:
            to_member(m_out, m_ret, mr_sems, n).wait_recv()
        for b in range(blocks):
            here, cols = pl.ds(b * rows, rows), pl.ds(h * width, width)
            dq_ref[here, cols] += m_ret[n] * factors[slot, b]

    units = blocks * heads
    stages = ((forward_member, -1), (forward_far, 1), (compute, 2), (return_far, 4), (return_near, 6), (finish, 8))
    for step in range(-1, max(count + 9, units)):
        if 0 <= step < units:
            own_unit(step)
        for stage_of, lag in stages:
            if 0 <= step - lag < count:
                stage_of(step - lag)
        if step == count + 1:
            dk_ref[...] = dk_ref[...] * scale

    for n in range(count):
        to_partner(local_of(n), x_arr, x_sems, n).wait_send()
        remote(x_arr, z_arr, z_sems, n, (far_to, member)).wait_send()
        remote(dq_item, z_ret, zr_sems, n, (far_from, member)).wait_send()
        to_partner(x_out, x_ret, xr_sems, n).wait_send()
        if items[n][0] != 0:
            to_member(stage, m_arr, m_sems, n).wait_send()
            to_member(m_out, m_ret, mr_sems, n).wait_send()


def settle(a_in, b_in, c_in, a_out, b_out, c_out, sems):
    pairs = ((a_in, a_out), (b_in, b_out), (c_in, c_out))
    copies = [pltpu.make_async_copy(x, y, sems.at[n]) for n, (x, y) in enumerate(pairs)]
    for copy in copies:
        copy.start()
    for copy in copies:
        copy.wait()


def body(queries, keys, values, outputs, out_grads, log_sums, block_lists):
    tokens, width_all = queries.shape
    heads = log_sums.shape[1]
    blocks = block_lists.shape[0]
    rows, width = tokens // blocks, width_all // heads
    groups, members = lax.axis_size("group"), lax.axis_size("member")
    sizes = (groups, members, heads, width, blocks, rows)
    vmem = pl.BlockSpec(memory_space=pltpu.VMEM)
    anywhere = pl.BlockSpec(memory_space=pl.ANY)
    count = members * heads
    packed = pltpu.VMEM((count, 2 * rows + 8, width), jnp.float32)
    terms = pltpu.VMEM((count, rows, width), jnp.float32)
    sems = pltpu.SemaphoreType.DMA((2, count))
    results = pl.pallas_call(
        functools.partial(kernel, sizes),
        out_shape=[jax.ShapeDtypeStruct((tokens, width_all), jnp.float32)] * 3,
        in_specs=[pl.BlockSpec(memory_space=pltpu.SMEM), anywhere, anywhere, anywhere, anywhere, anywhere, vmem],
        out_specs=[vmem] * 3,
        scratch_shapes=[
            pltpu.VMEM((tokens, width_all), jnp.float32),
            pltpu.VMEM((tokens, width_all), jnp.float32),
            pltpu.VMEM((tokens, width_all), jnp.float32),
            pltpu.VMEM((tokens, width_all), jnp.float32),
            pltpu.VMEM((tokens, width_all), jnp.float32),
            pltpu.VMEM((heads, tokens, 2 * width), jnp.bfloat16),
            pltpu.VMEM((heads, tokens, 2 * width), jnp.bfloat16),
            pltpu.VMEM((heads, 2 * width, tokens), jnp.bfloat16),
            pltpu.VMEM((blocks, heads, 8, width), jnp.float32),
            packed, packed, packed, packed,
            pltpu.VMEM((2 * rows + 8, width), jnp.float32),
            terms, terms, terms, terms, terms, terms,
            pltpu.SemaphoreType.DMA((5,)),
            sems, sems, sems, sems, sems, sems,
        ],
        compiler_params=pltpu.CompilerParams(
            collective_id=0, has_side_effects=True, vmem_limit_bytes=60 * 1024 * 1024
        ),
    )(block_lists, queries, keys, values, outputs, out_grads, log_sums.T)
    return pl.pallas_call(
        settle,
        out_shape=[jax.ShapeDtypeStruct((tokens, width_all), jnp.float32)] * 3,
        in_specs=[vmem] * 3,
        out_specs=[anywhere] * 3,
        scratch_shapes=[pltpu.SemaphoreType.DMA((3,))],
        compiler_params=pltpu.CompilerParams(vmem_limit_bytes=8 * 1024 * 1024),
    )(*results)


def solution(mesh):
    spec = P(("group", "member"), None)
    return jax.shard_map(
        body, mesh=mesh, in_specs=(spec,) * 7, out_specs=(spec,) * 3, check_vma=False
    )
```
